256 devices in a mesh: ctx: 4 (over y), row: 4 (over x_hi, core), col: 16 (over x_lo, z).
Axes of the slice: x: 4 (x_hi: 2, x_lo: 2; x = x_hi * 2 + x_lo), y: 4, z: 8, core: 2. Of those that a mesh axis runs over, the one named last changes fastest.
Arguments:
- events: bfloat16 [8192, 4096], P(('ctx', 'row'), 'col'), may hold values from -120 to 120
- domain_ids: int32 [8192], P(('ctx', 'row')), may hold values from 0 to 3
- block_order: int32 [4], replicated, may hold values from 0 to 3, each once
- query_weight: bfloat16 [4096, 4096], P('row', 'col'), may hold values from -0.09375 to 0.09375
- keyval_weight: bfloat16 [4096, 8, 2, 128], P('row'), may hold values from -0.09375 to 0.09375
- head_bias: float32 [32], P('col'), may hold values from -1.5 to 1.5
- out_weight: bfloat16 [4096, 4096], P('row', 'col'), may hold values from -0.09375 to 0.09375
Outputs:
- mixed: bfloat16 [8192, 4096], P(('ctx', 'row'), 'col')
The draws below stay inside these ranges and needn't reach their ends.
Inputs may be any that keep to these rules, and one draw needn't show every extreme that they name: `block_order`: each index of ctx holds 2048 consecutive events of one block; every place 0 to 3 is named once.
All inputs are finite; a program needn't handle non-finite values.
Results may differ from the reference program's by a relative error of at most 0.0075.
Values may be sent and summed in bfloat16 or wider, within the bound.
No kernel may reach another device: no remote copies, remote signals or barrier semaphores. Data moves between devices by JAX's collectives and lax.ppermute only.
A program may use at most 128 MiB of HBM per device.

```python
import math
import jax
import jax.numpy as jnp
from jax import lax

D = 4096
H = 32
KV = 8
HD = 128
DOMAINS = 4
GROUP_TOK = 2048
TOKENS = 8192
N_CTX = 4


def draw_events(key, part):
    key_base, key_rows, key_cols = jax.random.split(key, 3)
    raw_values = jnp.clip(jax.random.normal(key_base, (TOKENS, D), jnp.float32), -4.0, 4.0)
    row_scale = jnp.exp(jax.random.uniform(key_rows, (TOKENS, 1), jnp.float32, 0.0, math.log(10.0)))
    col_scale = jnp.exp(jax.random.uniform(key_cols, (1, D), jnp.float32, math.log(0.3), math.log(3.0)))
    return (raw_values * row_scale * col_scale).astype(jnp.bfloat16)


def touch_ends(entries, own_key, low, top_value):
    spot = [jax.random.randint(jax.random.fold_in(own_key, axis), (), 0, length) for axis, length in enumerate(entries.shape)]
    longest = entries.shape.index(max(entries.shape))
    next_to = spot[:longest] + [(spot[longest] + 1) % entries.shape[longest]] + spot[longest + 1:]
    return entries.at[tuple(spot)].set(low).at[tuple(next_to)].set(top_value)


def shard_levels(rng, dims, cuts, smallest, top_value):
    level, own = 1.0, jax.random.fold_in(rng, 6)
    for dim, parts in cuts:
        steps = jnp.exp(jax.random.uniform(jax.random.fold_in(own, dim), (parts,), jnp.float32, smallest / len(cuts), top_value / len(cuts)))
        level = level * jnp.repeat(steps, dims[dim] // parts).reshape([-1 if axis == dim else 1 for axis in range(len(dims))])
    return level


def centred(own_key, extent, spread, bound, pieces=(), held_as=jnp.bfloat16):
    values = jax.random.normal(own_key, extent, jnp.float32) * spread
    if len(pieces) > 0:
        values = shard_levels(own_key, extent, pieces, -0.22, 0.18) * values
    return jnp.clip(values, min=-bound, max=bound).astype(held_as)


def setup_inputs(seed: int = 0) -> dict:
    arg_keys = jax.random.split(jax.random.key(seed), 8)
    events = draw_events(jax.random.fold_in(arg_keys[7], 71), 0)
    domain_ids = touch_ends(jax.random.randint(arg_keys[1], (TOKENS,), 0, DOMAINS), jax.random.fold_in(arg_keys[1], 1), 0, DOMAINS - 1).astype(jnp.int32)
    block_order = jax.random.permutation(arg_keys[2], N_CTX).astype(jnp.int32)
    query_weight = centred(arg_keys[3], (D, H * HD), D ** -0.5, 0.09375, ((0, 4), (1, 16)))
    keyval_weight = centred(arg_keys[4], (D, KV, 2, HD), D ** -0.5, 0.09375, ((0, 4),))
    head_bias = jnp.clip(jax.random.uniform(arg_keys[5], (H,), jnp.float32, -1.5, 1.5) * shard_levels(arg_keys[5], (H,), ((0, 16),), -0.4, 0.0), -1.5, 1.5)
    out_weight = centred(arg_keys[6], (H * HD, D), (H * HD) ** -0.5, 0.09375, ((0, 4), (1, 16)))
    return {"events": events, "domain_ids": domain_ids, "block_order": block_order, "query_weight": query_weight, "keyval_weight": keyval_weight, "head_bias": head_bias, "out_weight": out_weight}


norm_eps = 1e-06

def reference(events, domain_ids, block_order, query_weight, keyval_weight, head_bias, out_weight):
    wide_events = events.astype(jnp.float32)
    normed = (wide_events * lax.rsqrt(lax.optimization_barrier(jnp.mean(wide_events * wide_events, axis=1, keepdims=True)) + norm_eps)).astype(jnp.bfloat16)
    queries = jnp.dot(normed, query_weight, preferred_element_type=jnp.float32).astype(jnp.bfloat16)
    queries = queries.reshape(TOKENS, H, HD)
    keyvals = jnp.dot(normed, keyval_weight.reshape(D, KV * 2 * HD), preferred_element_type=jnp.float32).astype(jnp.bfloat16)
    keyvals = keyvals.reshape(TOKENS, KV, 2, HD)
    storage = jnp.arange(TOKENS, dtype=jnp.int32)
    place = block_order[storage // GROUP_TOK] * GROUP_TOK + storage % GROUP_TOK
    inv_count = lax.rsqrt((place + 1).astype(jnp.float32))
    scale_factor = 1.0 / math.sqrt(HD)
    group_size = H // KV

    def one_head(head_index):
        query_head = lax.dynamic_index_in_dim(queries, head_index, 1, keepdims=False)
        pair = lax.dynamic_index_in_dim(keyvals, head_index // group_size, 1, keepdims=False)
        scores = jnp.dot(query_head, pair[:, 0, :].T, preferred_element_type=jnp.float32) * scale_factor
        same_domain = (domain_ids[:, None] == domain_ids[None, :]).astype(jnp.float32)
        scores = scores + lax.dynamic_index_in_dim(head_bias, head_index, 0, keepdims=False) * same_domain
        visible = place[None, :] <= place[:, None]
        weights = jnp.where(visible, jax.nn.silu(scores) * inv_count[:, None], 0.0).astype(jnp.bfloat16)
        return jnp.dot(weights, pair[:, 1, :], preferred_element_type=jnp.float32).astype(jnp.bfloat16)
    per_head = lax.map(one_head, jnp.arange(H, dtype=jnp.int32))
    attended = jnp.transpose(per_head, (1, 0, 2)).reshape(TOKENS, H * HD)
    return jnp.dot(attended, out_weight, preferred_element_type=jnp.float32).astype(jnp.bfloat16)
```

```python
import functools
import math

import jax
import jax.numpy as jnp
from jax import lax
from jax.experimental import pallas as pl
from jax.experimental.pallas import tpu as pltpu
from jax.sharding import Mesh
from jax.sharding import PartitionSpec as P

H = 32
KV = 8
HD = 128
D = 4096
NZ = 8
NY = 4
norm_eps = 1e-06
BF = jnp.bfloat16
F32 = jnp.float32

SWAP = [(0, 1), (1, 0)]
TAKE_0 = [(xl * 2 + xh, xh * 2 + xl) for xh in range(2) for xl in range(2)]
TAKE_1 = [(xl * 2 + 1 - xh, xh * 2 + xl) for xh in range(2) for xl in range(2)]


def shift(x, axis, size, by):
    return lax.ppermute(x, axis, [(i, (i + by) % size) for i in range(size)])


def ring(x):
    got = {0: x}
    up = down = x
    for s in range(1, 5):
        up = shift(up, "z", NZ, 1)
        got[s] = up
        if s < 4:
            down = shift(down, "z", NZ, -1)
            got[NZ - s] = down
    return [got[s] for s in range(NZ)]


def proj_kernel(with_squares, n_w, scal, *refs):
    xs = refs[:NZ]
    ws = refs[NZ : NZ + 2 * n_w]
    outs = refs[NZ + 2 * n_w :]
    keep, send = outs[0], outs[1]
    acc = outs[-1]
    z, core, flag = scal[0], scal[1], scal[2]
    width = acc.shape[1] // n_w
    squares = None
    for s in range(NZ):
        zz = lax.rem(z - s + NZ, NZ)
        off = pl.multiple_of(lax.rem(zz, 4) * 256, 256)
        here = zz // 4 == core
        x = xs[s][...]

        def add(which):
            for k in range(n_w):
                part = jnp.dot(
                    x, ws[2 * k + which][pl.ds(off, 256), :], preferred_element_type=F32
                )
                cols = slice(k * width, (k + 1) * width)
                if s == 0:
                    acc[:, cols] = part
                else:
                    acc[:, cols] += part

        pl.when(here)(functools.partial(add, 0))
        pl.when(jnp.logical_not(here))(functools.partial(add, 1))
        if with_squares:
            wide = x.astype(F32)
            sq = wide * wide
            hi = sq.astype(BF)
            lo = (sq - hi.astype(F32)).astype(BF)
            ones = jnp.ones((8, 256), BF)
            dims = (((1,), (1,)), ((), ()))
            row = lax.dot_general(ones, hi, dims, preferred_element_type=F32)
            row = row + lax.dot_general(ones, lo, dims, preferred_element_type=F32)
            squares = row if squares is None else squares + row
    half = acc.shape[1] // 2

    def write(first):
        mine = slice(0, half) if first else slice(half, 2 * half)
        other = slice(half, 2 * half) if first else slice(0, half)
        keep[...] = acc[:, mine]
        send[...] = acc[:, other].astype(BF)

    pl.when(flag == 0)(functools.partial(write, True))
    pl.when(flag != 0)(functools.partial(write, False))
    if with_squares:
        outs[2][...] = squares


def project(xs, ws, scal, with_squares=False):
    rows = xs[0].shape[0]
    n_w = len(ws) // 2
    total = n_w * ws[0].shape[1]
    vm = pl.BlockSpec(memory_space=pltpu.VMEM)
    out_shape = [
        jax.ShapeDtypeStruct((rows, total // 2), F32),
        jax.ShapeDtypeStruct((rows, total // 2), BF),
    ]
    if with_squares:
        out_shape.append(jax.ShapeDtypeStruct((8, rows), F32))
    return pl.pallas_call(
        functools.partial(proj_kernel, with_squares, n_w),
        out_shape=out_shape,
        in_specs=[pl.BlockSpec(memory_space=pltpu.SMEM)] + [vm] * (len(xs) + len(ws)),
        out_specs=[vm] * len(out_shape),
        scratch_shapes=[pltpu.VMEM((rows, total), F32)],
        name="project",
    )(scal, *xs, *ws)


def attend_kernel(n_blocks, scal, q_ref, qoh_ref, koh_ref, *refs):
    kvs = refs[:n_blocks]
    own_out, other_out, k_scr, v_scr, acc = refs[n_blocks:]
    rows = own_out.shape[0]
    for j in range(n_blocks):
        k_scr[j, :, :HD] = kvs[j][:, :HD]
        k_scr[j, :, HD:] = koh_ref[j]
        v_scr[j] = kvs[j][:, HD:]
    acc[...] = jnp.zeros_like(acc)

    def tile(g, j, diagonal):
        for h in range(2):
            q = jnp.concatenate([q_ref[g, :, h * HD : (h + 1) * HD], qoh_ref[g, h]], axis=1)
            u = lax.dot_general(
                q, k_scr[j], (((1,), (1,)), ((), ())), preferred_element_type=F32
            )
            w = u + u * jnp.tanh(u)
            if diagonal:
                t_at = lax.broadcasted_iota(jnp.int32, w.shape, 0)
                u_at = lax.broadcasted_iota(jnp.int32, w.shape, 1)
                w = jnp.where(u_at <= t_at, w, 0.0)
            acc[g, :, h * HD : (h + 1) * HD] += jnp.dot(
                w.astype(BF), v_scr[j], preferred_element_type=F32
            )

    tile(0, 0, True)

    def step(i, carry):
        g, j = i // n_blocks, lax.rem(i, n_blocks)

        @pl.when(scal[2 + j] < scal[g])
        def _():
            tile(g, j, False)

        return carry

    lax.fori_loop(0, 2 * n_blocks, step, 0)
    own_out[...] = acc[0]
    other_out[...] = acc[1].astype(BF)


def attend(scal, q, qoh, koh, kvs):
    rows = kvs[0].shape[0]
    n = len(kvs)
    vm = pl.BlockSpec(memory_space=pltpu.VMEM)
    return pl.pallas_call(
        functools.partial(attend_kernel, n),
        out_shape=[
            jax.ShapeDtypeStruct((rows, 2 * HD), F32),
            jax.ShapeDtypeStruct((rows, 2 * HD), BF),
        ],
        in_specs=[pl.BlockSpec(memory_space=pltpu.SMEM)] + [vm] * (3 + n),
        out_specs=[vm] * 2,
        scratch_shapes=[
            pltpu.VMEM((n, rows, 2 * HD), BF),
            pltpu.VMEM((n, rows, HD), BF),
            pltpu.VMEM((2, rows, 2 * HD), F32),
        ],
        name="attend",
    )(scal, q, qoh, koh, *kvs)


def shards(events, domain_ids, block_order, query_weight, keyval_weight, head_bias, out_weight):
    rows = events.shape[0]
    y, xh, core = lax.axis_index("y"), lax.axis_index("xh"), lax.axis_index("core")
    xl, z = lax.axis_index("xl"), lax.axis_index("z")
    chip_x = ("xh", "xl")

    group = z // 2
    pairs = [
        lax.dynamic_slice_in_dim(keyval_weight, group + 4 * b, 1, 1).reshape(-1, 2 * HD)
        for b in range(2)
    ]
    kvw = lax.ppermute(jnp.concatenate(pairs, axis=1), chip_x, TAKE_0)
    blocks = ring(events)
    kvw_other = lax.ppermute(kvw, "core", SWAP)
    qw = [lax.ppermute(query_weight, chip_x, take) for take in (TAKE_0, TAKE_1)]
    qw_other = [lax.ppermute(w, "core", SWAP) for w in qw]

    ids_other = lax.ppermute(domain_ids, "core", SWAP)
    ids_pair = jnp.stack([domain_ids, lax.ppermute(domain_ids, "xh", SWAP)])
    ids_keys = jnp.concatenate([ids_pair] + [shift(ids_pair, "y", NY, d) for d in (1, 3, 2)])
    lane = jnp.arange(HD, dtype=jnp.int32)
    koh = ((ids_keys[:, :, None] == lane % 4) & (lane < 8)).astype(BF)
    bias = 0.5 * head_bias
    high = lax.reduce_precision(bias, 8, 7)
    coef = jnp.where(lane < 4, high[:, None], jnp.where(lane < 8, (bias - high)[:, None], 0.0))
    ids_q = jnp.stack([domain_ids, ids_other])
    qoh = jnp.where(ids_q[:, None, :, None] == lane % 4, coef[None, :, None, :], 0.0).astype(BF)

    dy = jnp.array([0, 0, 1, 1, 3, 3, 2, 2], jnp.int32)
    dx = jnp.array([0, 1] * 4, jnp.int32)
    src_y = (y - dy) % NY
    at = jnp.sum(jnp.where(src_y[:, None] == jnp.arange(NY), block_order[None, :], 0), axis=1)
    key_at = at * 4 + (xh ^ dx) * 2 + core
    own_at = key_at[0]
    scal_a = jnp.concatenate([jnp.stack([own_at, own_at ^ 1]), key_at]).astype(jnp.int32)

    kv_keep, kv_send, squares = project(
        blocks, [kvw, kvw_other], jnp.stack([z, core, xl]), with_squares=True
    )
    kv_got = lax.ppermute(kv_send, "xl", SWAP)
    sq = squares[0]
    sq = sq + lax.ppermute(sq, "xl", SWAP)
    row_scale = lax.rsqrt(sq * (1.0 / D) + norm_eps)[:, None]
    kv = ((kv_keep + kv_got.astype(F32)) * row_scale).astype(BF)
    kv_x = lax.ppermute(kv, "xh", SWAP)
    kvs = [kv, kv_x]
    for d in (1, 3, 2):
        kvs.append(shift(kv, "y", NY, d))
        kvs.append(shift(kv_x, "y", NY, d))

    q_keep, q_send = project(
        blocks, [qw[0], qw_other[0], qw[1], qw_other[1]], jnp.stack([z, core, xl ^ xh])
    )
    q_got = lax.ppermute(q_send, "xl", SWAP)
    q = ((q_keep + q_got.astype(F32)) * (row_scale * (0.5 / math.sqrt(HD)))).astype(BF)
    q_both = jnp.stack([q, lax.ppermute(q, "core", SWAP)])

    ow = [lax.ppermute(out_weight, chip_x, take) for take in (TAKE_0, TAKE_1)]
    ow_other = [lax.ppermute(w, "core", SWAP) for w in ow]

    mine, theirs = attend(scal_a, q_both, qoh, koh, kvs)
    back = lax.ppermute(theirs, "core", SWAP)
    place = own_at * rows + jnp.arange(rows, dtype=jnp.int32)
    inv = lax.rsqrt((place + 1).astype(F32))[:, None]
    attended = ((mine + back.astype(F32)) * inv).astype(BF)

    o_keep, o_send = project(
        ring(attended), [ow[0], ow_other[0], ow[1], ow_other[1]], jnp.stack([z, core, xl ^ xh])
    )
    o_got = lax.ppermute(o_send, "xl", SWAP)
    return (o_keep + o_got.astype(F32)).astype(BF)


def solution(mesh):
    split = Mesh(mesh.devices.reshape(4, 2, 2, 2, 8), ("y", "xh", "core", "xl", "z"))
    r, c = ("y", "xh", "core"), ("xl", "z")
    w = ("xh", "core")
    return jax.shard_map(
        shards,
        mesh=split,
        in_specs=(P(r, c), P(r), P(), P(w, c), P(w, None, None, None), P(c), P(w, c)),
        out_specs=P(r, c),
        check_vma=False,
    )
```

```python
import functools
import math

import jax
import jax.numpy as jnp
from jax import lax
from jax.experimental import pallas as pl
from jax.experimental.pallas import tpu as pltpu
from jax.sharding import Mesh
from jax.sharding import PartitionSpec as P


HD = 128
D = 4096
NZ = 8
NY = 4
norm_eps = 1e-06
BF = jnp.bfloat16
F32 = jnp.float32

SWAP = [(0, 1), (1, 0)]
TAKE_0 = [(xl * 2 + xh, xh * 2 + xl) for xh in range(2) for xl in range(2)]
TAKE_1 = [(xl * 2 + 1 - xh, xh * 2 + xl) for xh in range(2) for xl in range(2)]


def shift(x, axis, size, by):
    return lax.ppermute(x, axis, [(i, (i + by) % size) for i in range(size)])


def after(x, *others):
    return lax.optimization_barrier((x, *others))[0]


def ring(x):
    got = {0: x}
    up = down = x
    for s in range(1, 4):
        up = got[s] = shift(up, "z", NZ, 1)
        down = got[NZ - s] = shift(down, "z", NZ, -1)
    pairs = [(c * NZ + i, c * NZ + (i + 1 - 2 * c) % NZ) for c in range(2) for i in range(NZ)]
    last = jnp.where(lax.axis_index("core") == 0, up, down)
    return [got[s] for s in range(NZ) if s != 4], lax.ppermute(last, ("core", "z"), pairs)


def proj_kernel(mode, with_squares, n_w, pick, scal, *refs):
    n_x = {"all": 8, "most": 7, "last": 1}[mode]
    xs, refs = refs[:n_x], refs[n_x:]
    n_ws = 4 if mode == "all" else 2 * n_w
    ws, refs = refs[:n_ws], refs[n_ws:]
    z, core = scal[0], scal[1]
    ones = jnp.ones((8, 256), BF)
    dims = (((1,), (1,)), ((), ()))

    def squares_of(x):
        wide = x.astype(F32)
        sq = wide * wide
        hi = sq.astype(BF)
        lo = (sq - hi.astype(F32)).astype(BF)
        return lax.dot_general(ones, hi, dims, preferred_element_type=F32) + lax.dot_general(
            ones, lo, dims, preferred_element_type=F32
        )

    def column(s):
        return pl.multiple_of(lax.rem(z - s + NZ, NZ) * 256, 256)

    def write(acc, keep, send):
        half = acc.shape[1] // 2

        def put(first):
            mine, other = slice(0, half), slice(half, 2 * half)
            if not first:
                mine, other = other, mine
            keep[...] = acc[:, mine]
            send[...] = acc[:, other].astype(BF)

        flag = scal[pick]
        pl.when(flag == 0)(functools.partial(put, True))
        pl.when(flag != 0)(functools.partial(put, False))

    if mode == "last":
        if with_squares:
            sums, old_sq, keep, send, new_sq, acc = refs
        else:
            sums, keep, send, acc = refs
        off = column(4)
        here = off // 1024 == core
        off = pl.multiple_of(lax.rem(off, 1024), 256)
        x = xs[0][...]

        def add(which):
            width = acc.shape[1] // n_w
            for k in range(n_w):
                cols = slice(k * width, (k + 1) * width)
                acc[:, cols] = sums[:, cols] + jnp.dot(
                    x, ws[2 * k + which][pl.ds(off, 256), :], preferred_element_type=F32
                )

        pl.when(here)(functools.partial(add, 0))
        pl.when(jnp.logical_not(here))(functools.partial(add, 1))
        if with_squares:
            new_sq[...] = old_sq[...] + squares_of(x)
        write(acc, keep, send)
        return

    x_scr = refs[-1]
    order = [s for s in range(NZ) if s != 4]
    for s, ref in zip(order, xs):
        x_scr[:, pl.ds(column(s), 256)] = ref[...]
    if mode == "all":
        x_scr[:, pl.ds(column(4), 256)] = xs[7][...]
        keep, send, acc = refs[0], refs[1], refs[-2]
        half = scal[14]
        acc[...] = sum(
            jnp.dot(
                x_scr[:, pl.ds(pl.multiple_of(c * 1024 + h * 512, 512), 512)],
                w[...],
                preferred_element_type=F32,
            )
            for w, c, h in zip(
                ws, (core, core, 1 - core, 1 - core), (half, 1 - half, half, 1 - half)
            )
        )
        write(acc, keep, send)
        return
    x_scr[:, pl.ds(column(4), 256)] = jnp.zeros((x_scr.shape[0], 256), BF)
    acc = refs[0]
    near = pl.multiple_of(core * 1024, 1024)
    far = pl.multiple_of((1 - core) * 1024, 1024)
    width = acc.shape[1] // n_w
    for k in range(n_w):
        acc[:, k * width : (k + 1) * width] = jnp.dot(
            x_scr[:, pl.ds(near, 1024)], ws[2 * k][...], preferred_element_type=F32
        ) + jnp.dot(x_scr[:, pl.ds(far, 1024)], ws[2 * k + 1][...], preferred_element_type=F32)
    if with_squares:
        refs[1][...] = sum(squares_of(ref[...]) for ref in xs)


VM = pl.BlockSpec(memory_space=pltpu.VMEM)
SM = pl.BlockSpec(memory_space=pltpu.SMEM)


def project_most(scal, xs, ws, with_squares):
    rows = xs[0].shape[0]
    n_w = len(ws) // 2
    total = n_w * ws[0].shape[1]
    out = [jax.ShapeDtypeStruct((rows, total), F32)]
    if with_squares:
        out.append(jax.ShapeDtypeStruct((8, rows), F32))
    return pl.pallas_call(
        functools.partial(proj_kernel, "most", with_squares, n_w, None),
        out_shape=out,
        in_specs=[SM] + [VM] * (len(xs) + len(ws)),
        out_specs=[VM] * len(out),
        scratch_shapes=[pltpu.VMEM((rows, 8 * 256), BF)],
        cost_estimate=pl.CostEstimate(
            flops=2 * rows * 1792 * total, transcendentals=0, bytes_accessed=8 * rows * total
        ),
        compiler_params=pltpu.CompilerParams(vmem_limit_bytes=PROJECT_VMEM),
        name="project_most",
    )(scal, *xs, *ws)


def project_last(scal, pick, last, ws, sums):
    rows = last.shape[0]
    n_w = len(ws) // 2
    total = n_w * ws[0].shape[1]
    out = [
        jax.ShapeDtypeStruct((rows, total // 2), F32),
        jax.ShapeDtypeStruct((rows, total // 2), BF),
    ]
    if len(sums) > 1:
        out.append(jax.ShapeDtypeStruct((8, rows), F32))
    return pl.pallas_call(
        functools.partial(proj_kernel, "last", len(sums) > 1, n_w, pick),
        out_shape=out,
        in_specs=[SM] + [VM] * (1 + len(ws) + len(sums)),
        out_specs=[VM] * len(out),
        scratch_shapes=[pltpu.VMEM((rows, total), F32)],
        compiler_params=pltpu.CompilerParams(vmem_limit_bytes=PROJECT_VMEM),
        name="project_last",
    )(scal, last, *ws, *sums)


def project_all(scal, pick, xs, last, ws):
    rows = last.shape[0]
    total = ws[0].shape[1]
    out = [
        jax.ShapeDtypeStruct((rows, total // 2), F32),
        jax.ShapeDtypeStruct((rows, total // 2), BF),
    ]
    return pl.pallas_call(
        functools.partial(proj_kernel, "all", False, 1, pick),
        out_shape=out,
        in_specs=[SM] + [VM] * (8 + len(ws)),
        out_specs=[VM] * len(out),
        scratch_shapes=[pltpu.VMEM((rows, total), F32), pltpu.VMEM((rows, 8 * 256), BF)],
        cost_estimate=pl.CostEstimate(
            flops=2 * rows * 2048 * total, transcendentals=0, bytes_accessed=8 * rows * total
        ),
        compiler_params=pltpu.CompilerParams(vmem_limit_bytes=PROJECT_VMEM),
        name="project_all",
    )(scal, *xs, last, *ws)


PROJECT_VMEM = 20 << 20
ATTEND_VMEM = 28 << 20


def attend_kernel(which, first, final, scal, q_ref, qoh_ref, koh_ref, *refs):
    n = len(which)
    kvs, refs = refs[:n], refs[n:]
    if not first:
        before, refs = refs[0], refs[1:]
    if final:
        own_out, other_out, k_scr, v_scr, acc = refs
    else:
        acc, k_scr, v_scr = refs
    for i in range(n):
        k_scr[i, :, :HD] = kvs[i][:, :HD]
        k_scr[i, :, HD:] = koh_ref[which[i]]
        v_scr[i] = kvs[i][:, HD:]
    if first:
        acc[...] = jnp.zeros_like(acc)
    else:
        acc[...] = before[...]

    def tile(g, i, diagonal):
        keys = k_scr[i]
        values = v_scr[i]
        for h in range(2):
            q = jnp.concatenate([q_ref[g, :, h * HD : (h + 1) * HD], qoh_ref[g, h]], axis=1)
            u = lax.dot_general(q, keys, (((1,), (1,)), ((), ())), preferred_element_type=F32)
            w = u + u * jnp.tanh(u)
            if diagonal:
                t_at = lax.broadcasted_iota(jnp.int32, w.shape, 0)
                u_at = lax.broadcasted_iota(jnp.int32, w.shape, 1)
                w = jnp.where(u_at <= t_at, w, 0.0)
            acc[g, :, h * HD : (h + 1) * HD] += jnp.dot(
                w.astype(BF), values, preferred_element_type=F32
            )

    if first:
        tile(0, 0, True)

        @pl.when(scal[6] < scal[5])
        def _():
            tile(1, 0, False)

    start = 1 if first else 0

    def step(i, carry):
        at = scal[6 + which[start]]
        for m in range(start + 1, n):
            at = jnp.where(i == m, scal[6 + which[m]], at)

        @pl.when(at < scal[4])
        def _():
            tile(0, i, False)
            tile(1, i, False)

        return carry

    lax.fori_loop(start, n, step, 0)
    if final:
        own_out[...] = acc[0]
        other_out[...] = acc[1].astype(BF)


def attend(scal, q, qoh, koh, kvs, which, before=None, final=False):
    rows = kvs[0].shape[0]
    n = len(kvs)
    sums = jax.ShapeDtypeStruct((2, rows, 2 * HD), F32)
    out = [sums]
    scratch = [pltpu.VMEM((n, rows, 2 * HD), BF), pltpu.VMEM((n, rows, HD), BF)]
    if final:
        out = [
            jax.ShapeDtypeStruct((rows, 2 * HD), F32),
            jax.ShapeDtypeStruct((rows, 2 * HD), BF),
        ]
        scratch.append(pltpu.VMEM((2, rows, 2 * HD), F32))
    extra = [] if before is None else [before]
    return pl.pallas_call(
        functools.partial(attend_kernel, which, before is None, final),
        out_shape=out,
        in_specs=[SM] + [VM] * (3 + n + len(extra)),
        out_specs=[VM] * len(out),
        scratch_shapes=scratch,
        cost_estimate=pl.CostEstimate(
            flops=n * 2 * 4 * 2 * rows * rows * 256, transcendentals=0, bytes_accessed=1 << 20
        ),
        compiler_params=pltpu.CompilerParams(vmem_limit_bytes=ATTEND_VMEM),
        name="attend",
    )(scal, q, qoh, koh, *kvs, *extra)


def shards(events, domain_ids, block_order, query_weight, keyval_weight, head_bias, out_weight):
    rows = events.shape[0]
    y, xh, core = lax.axis_index("y"), lax.axis_index("xh"), lax.axis_index("core")
    xl, z = lax.axis_index("xl"), lax.axis_index("z")
    chip_x = ("xh", "xl")

    xs, last = ring(events)
    pairs = [
        lax.dynamic_slice(
            keyval_weight, (0, z // 2 + 4 * b, z % 2, 0), (keyval_weight.shape[0], 1, 1, HD)
        ).reshape(-1, HD)
        for b in range(2)
    ]
    kvw = lax.ppermute(jnp.concatenate(pairs, axis=1), chip_x, TAKE_0)
    half = query_weight.shape[0] // 2
    qw_in = lax.dynamic_slice_in_dim(query_weight, (y % 2) * half, half, 0)
    qw = [lax.ppermute(qw_in, chip_x, t) for t in (TAKE_0, TAKE_1)]

    ids_other = lax.ppermute(domain_ids, "core", SWAP)
    ids_pair = jnp.stack([domain_ids, lax.ppermute(domain_ids, "xh", SWAP)])
    ids_keys = jnp.concatenate([ids_pair] + [shift(ids_pair, "y", NY, d) for d in (1, 3, 2)])
    lane = jnp.arange(HD, dtype=jnp.int32)
    koh = ((ids_keys[:, :, None] == lane % 4) & (lane < 8)).astype(BF)
    bias = 0.5 * head_bias
    high = lax.reduce_precision(bias, 8, 7)
    coef = jnp.where(lane < 4, high[:, None], jnp.where(lane < 8, (bias - high)[:, None], 0.0))
    ids_q = jnp.stack([domain_ids, ids_other])
    qoh = jnp.where(ids_q[:, None, :, None] == lane % 4, coef[None, :, None, :], 0.0).astype(BF)

    dy = jnp.array([0, 0, 1, 1, 3, 3, 2, 2], jnp.int32)
    dx = jnp.array([0, 1] * 4, jnp.int32)
    src_y = (y - dy) % NY
    at = jnp.sum(jnp.where(src_y[:, None] == jnp.arange(NY), block_order[None, :], 0), axis=1)
    key_at = at * 4 + (xh ^ dx) * 2 + core
    own_at = key_at[0]
    scal = jnp.concatenate([jnp.stack([z, core, xl, xl ^ xh, own_at, own_at ^ 1]), key_at, (y % 2)[None]])
    place = own_at * rows + jnp.arange(rows, dtype=jnp.int32)
    inv = lax.rsqrt((place + 1).astype(F32))[:, None]

    kvw_other = lax.ppermute(after(kvw, xs[3], xs[4], ids_keys, ids_other), "core", SWAP)
    kv_w = [kvw, kvw_other]
    sums = project_most(scal, xs, kv_w, True)
    kv_keep, kv_send, squares = project_last(scal, 2, last, kv_w, sums)
    kv_got = lax.ppermute(kv_send, "xl", SWAP)
    sq = squares[0]
    sq = sq + lax.ppermute(sq, "xl", SWAP)
    row_scale = lax.rsqrt(sq * (1.0 / D) + norm_eps)[:, None]
    mine = ((kv_keep + kv_got.astype(F32)) * row_scale).astype(BF)
    other = lax.ppermute(mine, "z", [(i, i ^ 1) for i in range(NZ)])
    even = z % 2 == 0
    kv = jnp.concatenate([jnp.where(even, mine, other), jnp.where(even, other, mine)], axis=1)
    kv_x = lax.ppermute(kv, "xh", SWAP)
    kv_up = shift(kv, "y", NY, 1)
    kv_down = shift(kv, "y", NY, -1)
    kv_far = shift(kv_up, "y", NY, 1)
    kv_x_up = shift(kv_x, "y", NY, 1)
    kv_x_down = shift(kv_x, "y", NY, -1)
    kv_x_far = shift(kv_x_down, "y", NY, -1)

    qw = jnp.concatenate(qw, axis=1)
    q_w = [qw, lax.ppermute(qw, "y", [(i, i ^ 1) for i in range(NY)])]
    q_w += [lax.ppermute(w, "core", SWAP) for w in q_w]
    q_keep, q_send = project_all(scal, 3, xs, last, q_w)
    q_got = lax.ppermute(q_send, "xl", SWAP)
    q = ((q_keep + q_got.astype(F32)) * (row_scale * (0.5 / math.sqrt(HD)))).astype(BF)
    q_both = jnp.stack([q, lax.ppermute(q, "core", SWAP)])

    ow = [lax.ppermute(out_weight, chip_x, t) for t in (TAKE_0, TAKE_1)]

    part = attend(scal, q_both, qoh, koh, [kv, kv_up, kv_down], (0, 2, 4))[0]
    part = attend(scal, q_both, qoh, koh, [kv_x, kv_far, kv_x_up, kv_x_down], (1, 6, 3, 5), part)[0]
    mine, theirs = attend(scal, q_both, qoh, koh, [kv_x_far], (7,), part, True)
    back = lax.ppermute(theirs, "core", SWAP)
    attended = ((mine + back.astype(F32)) * inv).astype(BF)

    hs, h_last = ring(attended)
    ow_other = [lax.ppermute(after(w, attended), "core", SWAP) for w in ow]
    o_w = [ow[0], ow_other[0], ow[1], ow_other[1]]
    sums = project_most(scal, hs, o_w, False)
    o_keep, o_send = project_last(scal, 3, h_last, o_w, sums)
    o_got = lax.ppermute(o_send, "xl", SWAP)
    return (o_keep + o_got.astype(F32)).astype(BF)


def solution(mesh):
    split = Mesh(mesh.devices.reshape(4, 2, 2, 2, 8), ("y", "xh", "core", "xl", "z"))
    r, c = ("y", "xh", "core"), ("xl", "z")
    w = ("xh", "core")
    return jax.shard_map(
        shards,
        mesh=split,
        in_specs=(P(r, c), P(r), P(), P(w, c), P(w, None, None, None), P(c), P(w, c)),
        out_specs=P(r, c),
        check_vma=False,
    )
```

```python
import functools
import math

import jax
import jax.numpy as jnp
from jax import lax
from jax.experimental import pallas as pl
from jax.experimental.pallas import tpu as pltpu
from jax.sharding import Mesh
from jax.sharding import PartitionSpec as P


HD = 128
D = 4096
NZ = 8
NY = 4
norm_eps = 1e-06
BF = jnp.bfloat16
F32 = jnp.float32

SWAP = [(0, 1), (1, 0)]
TAKE_0 = [(xl * 2 + xh, xh * 2 + xl) for xh in range(2) for xl in range(2)]
TAKE_1 = [(xl * 2 + 1 - xh, xh * 2 + xl) for xh in range(2) for xl in range(2)]


def shift(x, axis, size, by):
    return lax.ppermute(x, axis, [(i, (i + by) % size) for i in range(size)])


def ring(x):
    got = {0: x}
    up = down = x
    for s in range(1, 4):
        up = got[s] = shift(up, "z", NZ, 1)
        down = got[NZ - s] = shift(down, "z", NZ, -1)
    pairs = [(c * NZ + i, c * NZ + (i + 1 - 2 * c) % NZ) for c in range(2) for i in range(NZ)]
    last = jnp.where(lax.axis_index("core") == 0, up, down)
    return [got[s] for s in range(NZ) if s != 4], lax.ppermute(last, ("core", "z"), pairs)


def proj_kernel(mode, with_squares, n_w, pick, scal, *refs):
    n_x = {"all": 8, "most": 7, "last": 1}[mode]
    xs, refs = refs[:n_x], refs[n_x:]
    n_ws = 4 if mode == "all" else 2 * n_w
    ws, refs = refs[:n_ws], refs[n_ws:]
    z, core = scal[0], scal[1]
    ones = jnp.ones((8, 256), BF)
    dims = (((1,), (1,)), ((), ()))

    def squares_of(x):
        wide = x.astype(F32)
        sq = wide * wide
        hi = sq.astype(BF)
        lo = (sq - hi.astype(F32)).astype(BF)
        return lax.dot_general(ones, hi, dims, preferred_element_type=F32) + lax.dot_general(
            ones, lo, dims, preferred_element_type=F32
        )

    def column(s):
        return pl.multiple_of(lax.rem(z - s + NZ, NZ) * 256, 256)

    def write(acc, keep, send):
        half = acc.shape[1] // 2

        def put(first):
            mine, other = slice(0, half), slice(half, 2 * half)
            if not first:
                mine, other = other, mine
            keep[...] = acc[:, mine]
            send[: keep.shape[0], :] = acc[:, other].astype(BF)

        flag = scal[pick]
        pl.when(flag == 0)(functools.partial(put, True))
        pl.when(flag != 0)(functools.partial(put, False))

    if mode == "last":
        if with_squares:
            sums, old_sq, keep, send, new_sq, rows_scr, acc = refs
        else:
            sums, keep, send, acc = refs
        off = column(4)
        here = off // 1024 == core
        off = pl.multiple_of(lax.rem(off, 1024), 256)
        x = xs[0][...]

        def add(which):
            width = acc.shape[1] // n_w
            for k in range(n_w):
                cols = slice(k * width, (k + 1) * width)
                acc[:, cols] = sums[:, cols] + jnp.dot(
                    x, ws[2 * k + which][pl.ds(off, 256), :], preferred_element_type=F32
                )

        pl.when(here)(functools.partial(add, 0))
        pl.when(jnp.logical_not(here))(functools.partial(add, 1))
        write(acc, keep, send)
        if with_squares:
            rest = old_sq[...] + squares_of(x)
            new_sq[...] = rest
            rows_scr[...] = jnp.zeros_like(rows_scr)
            for t in range(3):
                term = rest.astype(BF).astype(F32)
                for k in range(4):
                    rows_scr[pl.ds(4 * t + k, 1), :] = term[:1, k * HD : (k + 1) * HD]
                rest = rest - term
            send[keep.shape[0] :, :] = rows_scr[...].astype(BF)
        return

    x_scr = refs[-1]
    order = [s for s in range(NZ) if s != 4]
    for s, ref in zip(order, xs):
        x_scr[:, pl.ds(column(s), 256)] = ref[...]
    if mode == "all":
        x_scr[:, pl.ds(column(4), 256)] = xs[7][...]
        keep, send, acc = refs[0], refs[1], refs[-2]
        half = scal[14]
        acc[...] = sum(
            jnp.dot(
                x_scr[:, pl.ds(pl.multiple_of(c * 1024 + h * 512, 512), 512)],
                w[...],
                preferred_element_type=F32,
            )
            for w, c, h in zip(
                ws, (core, core, 1 - core, 1 - core), (half, 1 - half, half, 1 - half)
            )
        )
        write(acc, keep, send)
        return
    x_scr[:, pl.ds(column(4), 256)] = jnp.zeros((x_scr.shape[0], 256), BF)
    acc = refs[0]
    near = pl.multiple_of(core * 1024, 1024)
    far = pl.multiple_of((1 - core) * 1024, 1024)
    width = acc.shape[1] // n_w
    for k in range(n_w):
        acc[:, k * width : (k + 1) * width] = jnp.dot(
            x_scr[:, pl.ds(near, 1024)], ws[2 * k][...], preferred_element_type=F32
        ) + jnp.dot(x_scr[:, pl.ds(far, 1024)], ws[2 * k + 1][...], preferred_element_type=F32)
    if with_squares:
        refs[1][...] = sum(squares_of(ref[...]) for ref in xs)


VM = pl.BlockSpec(memory_space=pltpu.VMEM)
SM = pl.BlockSpec(memory_space=pltpu.SMEM)


def project_most(scal, xs, ws, with_squares):
    rows = xs[0].shape[0]
    n_w = len(ws) // 2
    total = n_w * ws[0].shape[1]
    out = [jax.ShapeDtypeStruct((rows, total), F32)]
    if with_squares:
        out.append(jax.ShapeDtypeStruct((8, rows), F32))
    return pl.pallas_call(
        functools.partial(proj_kernel, "most", with_squares, n_w, None),
        out_shape=out,
        in_specs=[SM] + [VM] * (len(xs) + len(ws)),
        out_specs=[VM] * len(out),
        scratch_shapes=[pltpu.VMEM((rows, 8 * 256), BF)],
        cost_estimate=pl.CostEstimate(
            flops=2 * rows * 1792 * total, transcendentals=0, bytes_accessed=8 * rows * total
        ),
        compiler_params=pltpu.CompilerParams(vmem_limit_bytes=PROJECT_VMEM),
        name="project_most",
    )(scal, *xs, *ws)


def project_last(scal, pick, last, ws, sums):
    rows = last.shape[0]
    n_w = len(ws) // 2
    total = n_w * ws[0].shape[1]
    squares = len(sums) > 1
    out = [
        jax.ShapeDtypeStruct((rows, total // 2), F32),
        jax.ShapeDtypeStruct((rows + 16 if squares else rows, total // 2), BF),
    ]
    scratch = [pltpu.VMEM((rows, total), F32)]
    if squares:
        out.append(jax.ShapeDtypeStruct((8, rows), F32))
        scratch.insert(0, pltpu.VMEM((16, HD), F32))
    return pl.pallas_call(
        functools.partial(proj_kernel, "last", squares, n_w, pick),
        out_shape=out,
        in_specs=[SM] + [VM] * (1 + len(ws) + len(sums)),
        out_specs=[VM] * len(out),
        scratch_shapes=scratch,
        compiler_params=pltpu.CompilerParams(vmem_limit_bytes=PROJECT_VMEM),
        name="project_last",
    )(scal, last, *ws, *sums)


def project_all(scal, pick, xs, last, ws):
    rows = last.shape[0]
    total = ws[0].shape[1]
    out = [
        jax.ShapeDtypeStruct((rows, total // 2), F32),
        jax.ShapeDtypeStruct((rows, total // 2), BF),
    ]
    return pl.pallas_call(
        functools.partial(proj_kernel, "all", False, 1, pick),
        out_shape=out,
        in_specs=[SM] + [VM] * (8 + len(ws)),
        out_specs=[VM] * len(out),
        scratch_shapes=[pltpu.VMEM((rows, total), F32), pltpu.VMEM((rows, 8 * 256), BF)],
        cost_estimate=pl.CostEstimate(
            flops=2 * rows * 2048 * total, transcendentals=0, bytes_accessed=8 * rows * total
        ),
        compiler_params=pltpu.CompilerParams(vmem_limit_bytes=PROJECT_VMEM),
        name="project_all",
    )(scal, *xs, last, *ws)


PROJECT_VMEM = 20 << 20
ATTEND_VMEM = 28 << 20


def attend_kernel(which, first, final, scal, coef_ref, q_ref, q_other_ref, *refs):
    n = len(which)
    kvs, refs = refs[:n], refs[n:]
    if not first:
        before, refs = refs[0], refs[1:]
    if final:
        own_out, other_out, k_scr, v_scr, q_scr, acc = refs
    else:
        acc, k_scr, v_scr, q_scr = refs
    rows = acc.shape[1]

    def one_hot(ref, at):
        ids = ref[rows:, :].astype(F32)[at // 256 : at // 256 + 1, :]
        lane = lax.broadcasted_iota(jnp.int32, (16, 256), 0)
        hot = (ids == (lane % 4).astype(F32)) & (lane < 8)
        unit = lax.broadcasted_iota(jnp.int32, (16, HD), 0) == lax.broadcasted_iota(
            jnp.int32, (16, HD), 1
        )
        return lax.dot_general(
            hot.astype(F32).astype(BF),
            unit.astype(F32).astype(BF),
            (((0,), (0,)), ((), ())),
            preferred_element_type=F32,
        )

    for i in range(n):
        k_scr[i, :, :HD] = kvs[i][:rows, :HD]
        for at in range(0, rows, 256):
            k_scr[i, at : at + 256, HD:] = one_hot(kvs[i], at).astype(BF)
        v_scr[i] = kvs[i][:rows, HD:]
    for g, ref in enumerate((q_ref, q_other_ref)):
        for at in range(0, rows, 256):
            hot = one_hot(ref, at)
            for h in range(2):
                q_scr[g, h, at : at + 256, HD:] = (hot * coef_ref[h : h + 1, :]).astype(BF)
        for h in range(2):
            q_scr[g, h, :, :HD] = ref[:rows, h * HD : (h + 1) * HD]
    if first:
        acc[...] = jnp.zeros_like(acc)
    else:
        acc[...] = before[...]

    def tile(g, i, ahead=None):
        keys = k_scr[i]
        values = v_scr[i]
        for h in range(2):
            u = lax.dot_general(
                q_scr[g, h], keys, (((1,), (1,)), ((), ())), preferred_element_type=F32
            )
            w = u + u * jnp.tanh(u)
            if ahead is not None:
                t_at = lax.broadcasted_iota(jnp.int32, w.shape, 0)
                u_at = lax.broadcasted_iota(jnp.int32, w.shape, 1)
                w = jnp.where(u_at - t_at <= ahead, w, 0.0)
            acc[g, :, h * HD : (h + 1) * HD] += jnp.dot(
                w.astype(BF), values, preferred_element_type=F32
            )

    def place_of(i):
        at = scal[6 + which[0]]
        for m in range(1, n):
            at = jnp.where(i == m, scal[6 + which[m]], at)
        return at

    if first:

        def one(k, carry):
            g, i = k // n, lax.rem(k, n)
            own = k == 0

            @pl.when(jnp.logical_or(own, place_of(i) < scal[4 + g]))
            def _():
                tile(g, i, jnp.where(own, 0, rows))

            return carry

        lax.fori_loop(0, 2 * n, one, 0)
    else:

        def both(i, carry):
            @pl.when(place_of(i) < scal[4])
            def _():
                tile(0, i)
                tile(1, i)

            return carry

        lax.fori_loop(0, n, both, 0)
    if final:
        own_out[...] = acc[0]
        other_out[...] = acc[1].astype(BF)


def attend(scal, coef, q, q_other, kvs, which, before=None, final=False):
    rows = q.shape[0] - 16
    n = len(kvs)
    sums = jax.ShapeDtypeStruct((2, rows, 2 * HD), F32)
    out = [sums]
    scratch = [
        pltpu.VMEM((n, rows, 2 * HD), BF),
        pltpu.VMEM((n, rows, HD), BF),
        pltpu.VMEM((2, 2, rows, 2 * HD), BF),
    ]
    if final:
        out = [
            jax.ShapeDtypeStruct((rows, 2 * HD), F32),
            jax.ShapeDtypeStruct((rows, 2 * HD), BF),
        ]
        scratch.append(pltpu.VMEM((2, rows, 2 * HD), F32))
    extra = [] if before is None else [before]
    return pl.pallas_call(
        functools.partial(attend_kernel, which, before is None, final),
        out_shape=out,
        in_specs=[SM] + [VM] * (3 + n + len(extra)),
        out_specs=[VM] * len(out),
        scratch_shapes=scratch,
        cost_estimate=pl.CostEstimate(
            flops=n * 2 * 4 * 2 * rows * rows * 256, transcendentals=0, bytes_accessed=1 << 20
        ),
        compiler_params=pltpu.CompilerParams(vmem_limit_bytes=ATTEND_VMEM),
        name="attend",
    )(scal, coef, q, q_other, *kvs, *extra)


def shards(events, domain_ids, block_order, query_weight, keyval_weight, head_bias, out_weight):
    rows = events.shape[0]
    y, xh, core = lax.axis_index("y"), lax.axis_index("xh"), lax.axis_index("core")
    xl, z = lax.axis_index("xl"), lax.axis_index("z")
    chip_x = ("xh", "xl")

    xs, last = ring(events)
    pairs = [
        lax.dynamic_slice(
            keyval_weight, (0, z // 2 + 4 * b, z % 2, 0), (keyval_weight.shape[0], 1, 1, HD)
        ).reshape(-1, HD)
        for b in range(2)
    ]
    kvw = lax.ppermute(jnp.concatenate(pairs, axis=1), chip_x, TAKE_0)
    half = query_weight.shape[0] // 2
    qw_in = lax.dynamic_slice_in_dim(query_weight, (y % 2) * half, half, 0)
    qw = [lax.ppermute(qw_in, chip_x, t) for t in (TAKE_0, TAKE_1)]

    ids = jnp.pad(domain_ids.astype(BF).reshape(2, 256), ((0, 14), (0, 0)))
    lane = jnp.arange(HD, dtype=jnp.int32)
    bias = 0.5 * head_bias
    high = lax.reduce_precision(bias, 8, 7)
    coef = jnp.where(lane < 4, high[:, None], jnp.where(lane < 8, (bias - high)[:, None], 0.0))

    dy = jnp.array([0, 0, 1, 1, 3, 3, 2, 2], jnp.int32)
    dx = jnp.array([0, 1] * 4, jnp.int32)
    src_y = (y - dy) % NY
    at = jnp.sum(jnp.where(src_y[:, None] == jnp.arange(NY), block_order[None, :], 0), axis=1)
    key_at = at * 4 + (xh ^ dx) * 2 + core
    own_at = key_at[0]
    scal = jnp.concatenate([jnp.stack([z, core, xl, xl ^ xh, own_at, own_at ^ 1]), key_at, (y % 2)[None]])
    place = own_at * rows + jnp.arange(rows, dtype=jnp.int32)
    inv = lax.rsqrt((place + 1).astype(F32))[:, None]

    kvw_other = lax.ppermute(kvw, "core", SWAP)
    kv_w = [kvw, kvw_other]
    sums = project_most(scal, xs, kv_w, True)
    kv_keep, kv_send, squares = project_last(scal, 2, last, kv_w, sums)
    kv_got = lax.ppermute(kv_send, "xl", SWAP)
    sq = squares[0] + kv_got[rows : rows + 12].astype(F32).reshape(3, rows).sum(axis=0)
    row_scale = lax.rsqrt(sq * (1.0 / D) + norm_eps)[:, None]
    mine = ((kv_keep + kv_got[:rows].astype(F32)) * row_scale).astype(BF)
    other = lax.ppermute(mine, "z", [(i, i ^ 1) for i in range(NZ)])
    even = z % 2 == 0
    kv = jnp.concatenate([jnp.where(even, mine, other), jnp.where(even, other, mine)], axis=1)
    kv = jnp.concatenate([kv, ids], axis=0)
    kv_x = lax.ppermute(kv, "xh", SWAP)
    kv_up = shift(kv, "y", NY, 1)
    kv_down = shift(kv, "y", NY, -1)
    kv_far = shift(kv_up, "y", NY, 1)
    kv_x_up = shift(kv_x, "y", NY, 1)
    kv_x_down = shift(kv_x, "y", NY, -1)
    kv_x_far = shift(kv_x_down, "y", NY, -1)

    qw = jnp.concatenate(qw, axis=1)
    q_w = [qw, lax.ppermute(qw, "y", [(i, i ^ 1) for i in range(NY)])]
    q_w += [lax.ppermute(w, "core", SWAP) for w in q_w]
    q_keep, q_send = project_all(scal, 3, xs, last, q_w)
    q_got = lax.ppermute(q_send, "xl", SWAP)
    q = ((q_keep + q_got.astype(F32)) * (row_scale * (0.5 / math.sqrt(HD)))).astype(BF)
    q = jnp.concatenate([q, lax.optimization_barrier(ids)], axis=0)
    q_other = lax.ppermute(q, "core", SWAP)

    ow = [lax.ppermute(out_weight, chip_x, t) for t in (TAKE_0, TAKE_1)]

    part = attend(scal, coef, q, q_other, [kv, kv_up, kv_down], (0, 2, 4))[0]
    part = attend(scal, coef, q, q_other, [kv_x, kv_far, kv_x_up, kv_x_down], (1, 6, 3, 5), part)[0]
    mine, theirs = attend(scal, coef, q, q_other, [kv_x_far], (7,), part, True)
    back = lax.ppermute(theirs, "core", SWAP)
    attended = ((mine + back.astype(F32)) * inv).astype(BF)

    hs, h_last = ring(attended)
    ow_other = [lax.ppermute(w, "core", SWAP) for w in ow]
    o_w = [ow[0], ow_other[0], ow[1], ow_other[1]]
    sums = project_most(scal, hs, o_w, False)
    o_keep, o_send = project_last(scal, 3, h_last, o_w, sums)
    o_got = lax.ppermute(o_send, "xl", SWAP)
    return (o_keep + o_got.astype(F32)).astype(BF)


def solution(mesh):
    split = Mesh(mesh.devices.reshape(4, 2, 2, 2, 8), ("y", "xh", "core", "xl", "z"))
    r, c = ("y", "xh", "core"), ("xl", "z")
    w = ("xh", "core")
    return jax.shard_map(
        shards,
        mesh=split,
        in_specs=(P(r, c), P(r), P(), P(w, c), P(w, None, None, None), P(c), P(w, c)),
        out_specs=P(r, c),
        check_vma=False,
    )
```

```python
import functools
import math

import jax
import jax.numpy as jnp
from jax import lax
from jax.experimental import pallas as pl
from jax.experimental.pallas import tpu as pltpu
from jax.sharding import Mesh
from jax.sharding import PartitionSpec as P


HD = 128
D = 4096
NZ = 8
NY = 4
norm_eps = 1e-06
BF = jnp.bfloat16
F32 = jnp.float32

SWAP = [(0, 1), (1, 0)]
TAKE_0 = [(xl * 2 + xh, xh * 2 + xl) for xh in range(2) for xl in range(2)]
TAKE_1 = [(xl * 2 + 1 - xh, xh * 2 + xl) for xh in range(2) for xl in range(2)]


def shift(x, axis, size, by):
    return lax.ppermute(x, axis, [(i, (i + by) % size) for i in range(size)])


def ring(x):
    got = {0: x}
    up = down = x
    for s in range(1, 4):
        up = got[s] = shift(up, "z", NZ, 1)
        down = got[NZ - s] = shift(down, "z", NZ, -1)
    pairs = [(c * NZ + i, c * NZ + (i + 1 - 2 * c) % NZ) for c in range(2) for i in range(NZ)]
    last = jnp.where(lax.axis_index("core") == 0, up, down)
    return [got[s] for s in range(NZ) if s != 4], lax.ppermute(last, ("core", "z"), pairs)


def proj_kernel(mode, with_squares, n_w, pick, scal, *refs):
    n_x = {"all": 8, "most": 7, "last": 1}[mode]
    xs, refs = refs[:n_x], refs[n_x:]
    n_ws = 4 if mode == "all" else 2 * n_w
    ws, refs = refs[:n_ws], refs[n_ws:]
    z, core = scal[0], scal[1]
    ones = jnp.ones((8, 256), BF)
    dims = (((1,), (1,)), ((), ()))

    def squares_of(x):
        wide = x.astype(F32)
        sq = wide * wide
        hi = sq.astype(BF)
        lo = (sq - hi.astype(F32)).astype(BF)
        return lax.dot_general(ones, hi, dims, preferred_element_type=F32) + lax.dot_general(
            ones, lo, dims, preferred_element_type=F32
        )

    def column(s):
        return pl.multiple_of(lax.rem(z - s + NZ, NZ) * 256, 256)

    def write(acc, keep, send):
        half = acc.shape[1] // 2

        def put(first):
            mine, other = slice(0, half), slice(half, 2 * half)
            if not first:
                mine, other = other, mine
            keep[...] = acc[:, mine]
            send[: keep.shape[0], :] = acc[:, other].astype(BF)

        flag = scal[pick]
        pl.when(flag == 0)(functools.partial(put, True))
        pl.when(flag != 0)(functools.partial(put, False))

    if mode == "last":
        if with_squares:
            sums, old_sq, keep, send, new_sq, rows_scr, acc = refs
        else:
            sums, keep, send, acc = refs
        off = column(4)
        here = off // 1024 == core
        off = pl.multiple_of(lax.rem(off, 1024), 256)
        x = xs[0][...]

        def add(which):
            width = acc.shape[1] // n_w
            for k in range(n_w):
                cols = slice(k * width, (k + 1) * width)
                acc[:, cols] = sums[:, cols] + jnp.dot(
                    x, ws[2 * k + which][pl.ds(off, 256), :], preferred_element_type=F32
                )

        pl.when(here)(functools.partial(add, 0))
        pl.when(jnp.logical_not(here))(functools.partial(add, 1))
        write(acc, keep, send)
        if with_squares:
            rest = old_sq[...] + squares_of(x)
            new_sq[...] = rest
            rows_scr[...] = jnp.zeros_like(rows_scr)
            for t in range(3):
                term = rest.astype(BF).astype(F32)
                for k in range(4):
                    rows_scr[pl.ds(4 * t + k, 1), :] = term[:1, k * HD : (k + 1) * HD]
                rest = rest - term
            send[keep.shape[0] :, :] = rows_scr[...].astype(BF)
        return

    x_scr = refs[-1]
    order = [s for s in range(NZ) if s != 4]
    for s, ref in zip(order, xs):
        x_scr[:, pl.ds(column(s), 256)] = ref[...]
    if mode == "all":
        x_scr[:, pl.ds(column(4), 256)] = xs[7][...]
        keep, send, acc = refs[0], refs[1], refs[-2]
        half = scal[14]
        acc[...] = sum(
            jnp.dot(
                x_scr[:, pl.ds(pl.multiple_of(c * 1024 + h * 512, 512), 512)],
                w[...],
                preferred_element_type=F32,
            )
            for w, c, h in zip(
                ws, (core, core, 1 - core, 1 - core), (half, 1 - half, half, 1 - half)
            )
        )
        write(acc, keep, send)
        return
    x_scr[:, pl.ds(column(4), 256)] = jnp.zeros((x_scr.shape[0], 256), BF)
    acc = refs[0]
    near = pl.multiple_of(core * 1024, 1024)
    far = pl.multiple_of((1 - core) * 1024, 1024)
    width = acc.shape[1] // n_w
    for k in range(n_w):
        acc[:, k * width : (k + 1) * width] = jnp.dot(
            x_scr[:, pl.ds(near, 1024)], ws[2 * k][...], preferred_element_type=F32
        ) + jnp.dot(x_scr[:, pl.ds(far, 1024)], ws[2 * k + 1][...], preferred_element_type=F32)
    if with_squares:
        refs[1][...] = sum(squares_of(ref[...]) for ref in xs)


VM = pl.BlockSpec(memory_space=pltpu.VMEM)
SM = pl.BlockSpec(memory_space=pltpu.SMEM)


def project_most(scal, xs, ws, with_squares):
    rows = xs[0].shape[0]
    n_w = len(ws) // 2
    total = n_w * ws[0].shape[1]
    out = [jax.ShapeDtypeStruct((rows, total), F32)]
    if with_squares:
        out.append(jax.ShapeDtypeStruct((8, rows), F32))
    return pl.pallas_call(
        functools.partial(proj_kernel, "most", with_squares, n_w, None),
        out_shape=out,
        in_specs=[SM] + [VM] * (len(xs) + len(ws)),
        out_specs=[VM] * len(out),
        scratch_shapes=[pltpu.VMEM((rows, 8 * 256), BF)],
        cost_estimate=pl.CostEstimate(
            flops=2 * rows * 1792 * total, transcendentals=0, bytes_accessed=8 * rows * total
        ),
        compiler_params=pltpu.CompilerParams(vmem_limit_bytes=PROJECT_VMEM),
        name="project_most",
    )(scal, *xs, *ws)


def project_last(scal, pick, last, ws, sums):
    rows = last.shape[0]
    n_w = len(ws) // 2
    total = n_w * ws[0].shape[1]
    squares = len(sums) > 1
    out = [
        jax.ShapeDtypeStruct((rows, total // 2), F32),
        jax.ShapeDtypeStruct((rows + 16 if squares else rows, total // 2), BF),
    ]
    scratch = [pltpu.VMEM((rows, total), F32)]
    if squares:
        out.append(jax.ShapeDtypeStruct((8, rows), F32))
        scratch.insert(0, pltpu.VMEM((16, HD), F32))
    return pl.pallas_call(
        functools.partial(proj_kernel, "last", squares, n_w, pick),
        out_shape=out,
        in_specs=[SM] + [VM] * (1 + len(ws) + len(sums)),
        out_specs=[VM] * len(out),
        scratch_shapes=scratch,
        compiler_params=pltpu.CompilerParams(vmem_limit_bytes=PROJECT_VMEM),
        name="project_last",
    )(scal, last, *ws, *sums)


def project_all(scal, pick, xs, last, ws):
    rows = last.shape[0]
    total = ws[0].shape[1]
    out = [
        jax.ShapeDtypeStruct((rows, total // 2), F32),
        jax.ShapeDtypeStruct((rows, total // 2), BF),
    ]
    return pl.pallas_call(
        functools.partial(proj_kernel, "all", False, 1, pick),
        out_shape=out,
        in_specs=[SM] + [VM] * (8 + len(ws)),
        out_specs=[VM] * len(out),
        scratch_shapes=[pltpu.VMEM((rows, total), F32), pltpu.VMEM((rows, 8 * 256), BF)],
        cost_estimate=pl.CostEstimate(
            flops=2 * rows * 2048 * total, transcendentals=0, bytes_accessed=8 * rows * total
        ),
        compiler_params=pltpu.CompilerParams(vmem_limit_bytes=PROJECT_VMEM),
        name="project_all",
    )(scal, *xs, last, *ws)


PROJECT_VMEM = 10 << 20
ATTEND_VMEM = 16 << 20


def attend_kernel(which, first, final, scal, *refs):
    n = len(which)
    if first:
        coef_ref, q_ref, q_other_ref, *refs = refs
    else:
        q_scr, before, *refs = refs
    kvs, refs = refs[:n], refs[n:]
    if first:
        acc, q_scr, k_scr, v_scr = refs
    elif final:
        own_out, other_out, k_scr, v_scr, acc = refs
    else:
        acc, k_scr, v_scr = refs
    rows = acc.shape[1]

    def one_hot(ref, at):
        ids = ref[rows:, :].astype(F32)[at // 256 : at // 256 + 1, :]
        lane = lax.broadcasted_iota(jnp.int32, (16, 256), 0)
        hot = (ids == (lane % 4).astype(F32)) & (lane < 8)
        unit = lax.broadcasted_iota(jnp.int32, (16, HD), 0) == lax.broadcasted_iota(
            jnp.int32, (16, HD), 1
        )
        return lax.dot_general(
            hot.astype(F32).astype(BF),
            unit.astype(F32).astype(BF),
            (((0,), (0,)), ((), ())),
            preferred_element_type=F32,
        )

    for i in range(n):
        k_scr[i, :, :HD] = kvs[i][:rows, :HD]
        for at in range(0, rows, 256):
            k_scr[i, at : at + 256, HD:] = one_hot(kvs[i], at).astype(BF)
        v_scr[i] = kvs[i][:rows, HD:]
    if first:
        for g, ref in enumerate((q_ref, q_other_ref)):
            for at in range(0, rows, 256):
                hot = one_hot(ref, at)
                for h in range(2):
                    q_scr[g, h, at : at + 256, HD:] = (hot * coef_ref[h : h + 1, :]).astype(BF)
            for h in range(2):
                q_scr[g, h, :, :HD] = ref[:rows, h * HD : (h + 1) * HD]
        acc[...] = jnp.zeros_like(acc)
    else:
        acc[...] = before[...]

    def tile(g, i, ahead=None):
        keys = k_scr[i]
        values = v_scr[i]
        for h in range(2):
            u = lax.dot_general(
                q_scr[g, h], keys, (((1,), (1,)), ((), ())), preferred_element_type=F32
            )
            w = u + u * jnp.tanh(u)
            if ahead is not None:
                t_at = lax.broadcasted_iota(jnp.int32, w.shape, 0)
                u_at = lax.broadcasted_iota(jnp.int32, w.shape, 1)
                w = jnp.where(u_at - t_at <= ahead, w, 0.0)
            acc[g, :, h * HD : (h + 1) * HD] += jnp.dot(
                w.astype(BF), values, preferred_element_type=F32
            )

    def place_of(i):
        at = scal[6 + which[0]]
        for m in range(1, n):
            at = jnp.where(i == m, scal[6 + which[m]], at)
        return at

    if first:

        def one(k, carry):
            g, i = k // n, lax.rem(k, n)

            @pl.when(jnp.logical_or(k == 0, place_of(i) < scal[4 + g]))
            def _():
                tile(g, i, jnp.where(k == 0, 0, rows))

            return carry

        lax.fori_loop(0, 2 * n, one, 0)
    else:

        def both(i, carry):
            @pl.when(place_of(i) < scal[4])
            def _():
                tile(0, i)
                tile(1, i)

            return carry

        lax.fori_loop(0, n, both, 0)
    if final:
        own_out[...] = acc[0]
        other_out[...] = acc[1].astype(BF)


def attend(scal, queries, kvs, which, before=None, final=False):
    rows = kvs[0].shape[0] - 16
    n = len(kvs)
    first = before is None
    out = [jax.ShapeDtypeStruct((2, rows, 2 * HD), F32)]
    scratch = [pltpu.VMEM((n, rows, 2 * HD), BF), pltpu.VMEM((n, rows, HD), BF)]
    if first:
        out.append(jax.ShapeDtypeStruct((2, 2, rows, 2 * HD), BF))
    if final:
        out = [
            jax.ShapeDtypeStruct((rows, 2 * HD), F32),
            jax.ShapeDtypeStruct((rows, 2 * HD), BF),
        ]
        scratch.append(pltpu.VMEM((2, rows, 2 * HD), F32))
    ins = [*queries] if first else [*queries, before]
    return pl.pallas_call(
        functools.partial(attend_kernel, which, first, final),
        out_shape=out,
        in_specs=[SM] + [VM] * (len(ins) + n),
        out_specs=[VM] * len(out),
        scratch_shapes=scratch,
        cost_estimate=pl.CostEstimate(
            flops=n * 2 * 4 * 2 * rows * rows * 256, transcendentals=0, bytes_accessed=1 << 20
        ),
        compiler_params=pltpu.CompilerParams(vmem_limit_bytes=ATTEND_VMEM),
        name="attend",
    )(scal, *ins, *kvs)


def shards(events, domain_ids, block_order, query_weight, keyval_weight, head_bias, out_weight):
    rows = events.shape[0]
    y, xh, core = lax.axis_index("y"), lax.axis_index("xh"), lax.axis_index("core")
    xl, z = lax.axis_index("xl"), lax.axis_index("z")
    chip_x = ("xh", "xl")

    xs, last = ring(events)
    pairs = [
        lax.dynamic_slice(
            keyval_weight, (0, z // 2 + 4 * b, z % 2, 0), (keyval_weight.shape[0], 1, 1, HD)
        ).reshape(-1, HD)
        for b in range(2)
    ]
    kvw = lax.ppermute(jnp.concatenate(pairs, axis=1), chip_x, TAKE_0)
    half = query_weight.shape[0] // 2
    qw_in = lax.dynamic_slice_in_dim(query_weight, (y % 2) * half, half, 0)
    qw = [lax.ppermute(qw_in, chip_x, t) for t in (TAKE_0, TAKE_1)]

    ids = jnp.pad(domain_ids.astype(BF).reshape(2, 256), ((0, 14), (0, 0)))
    lane = jnp.arange(HD, dtype=jnp.int32)
    bias = 0.5 * head_bias
    high = lax.reduce_precision(bias, 8, 7)
    coef = jnp.where(lane < 4, high[:, None], jnp.where(lane < 8, (bias - high)[:, None], 0.0))

    dy = jnp.array([0, 0, 1, 1, 3, 3, 2, 2], jnp.int32)
    dx = jnp.array([0, 1] * 4, jnp.int32)
    src_y = (y - dy) % NY
    at = jnp.sum(jnp.where(src_y[:, None] == jnp.arange(NY), block_order[None, :], 0), axis=1)
    key_at = at * 4 + (xh ^ dx) * 2 + core
    own_at = key_at[0]
    scal = jnp.concatenate([jnp.stack([z, core, xl, xl ^ xh, own_at, own_at ^ 1]), key_at, (y % 2)[None]])
    place = own_at * rows + jnp.arange(rows, dtype=jnp.int32)
    inv = lax.rsqrt((place + 1).astype(F32))[:, None]

    kvw_other = lax.ppermute(kvw, "core", SWAP)
    kv_w = [kvw, kvw_other]
    sums = project_most(scal, xs, kv_w, True)
    kv_keep, kv_send, squares = project_last(scal, 2, last, kv_w, sums)
    kv_got = lax.ppermute(kv_send, "xl", SWAP)
    sq = squares[0] + kv_got[rows : rows + 12].astype(F32).reshape(3, rows).sum(axis=0)
    row_scale = lax.rsqrt(sq * (1.0 / D) + norm_eps)[:, None]
    mine = ((kv_keep + kv_got[:rows].astype(F32)) * row_scale).astype(BF)
    other = lax.ppermute(mine, "z", [(i, i ^ 1) for i in range(NZ)])
    even = z % 2 == 0
    kv = jnp.concatenate([jnp.where(even, mine, other), jnp.where(even, other, mine)], axis=1)
    kv = jnp.concatenate([kv, ids], axis=0)
    kv_x = lax.ppermute(kv, "xh", SWAP)
    kv_up = shift(kv, "y", NY, 1)
    kv_down = shift(kv, "y", NY, -1)
    kv_far = shift(kv_up, "y", NY, 1)
    kv_x_up = shift(kv_x, "y", NY, 1)
    kv_x_down = shift(kv_x, "y", NY, -1)
    kv_x_far = shift(kv_x_down, "y", NY, -1)

    qw = jnp.concatenate(lax.optimization_barrier((*qw, kv_send))[:2], axis=1)
    q_w = [qw, lax.ppermute(qw, "y", [(i, i ^ 1) for i in range(NY)])]
    q_w += [lax.ppermute(w, "core", SWAP) for w in q_w]
    q_keep, q_send = project_all(scal, 3, xs, last, q_w)
    q_got = lax.ppermute(q_send, "xl", SWAP)
    q = ((q_keep + q_got.astype(F32)) * (row_scale * (0.5 / math.sqrt(HD)))).astype(BF)
    q = jnp.concatenate([q, lax.optimization_barrier(ids)], axis=0)
    q_other = lax.ppermute(q, "core", SWAP)

    ow = [lax.ppermute(out_weight, chip_x, t) for t in (TAKE_0, TAKE_1)]

    part, full = attend(scal, (coef, q, q_other), [kv, kv_up, kv_down], (0, 2, 4))
    rest = [kv_x, kv_far, kv_x_up, kv_x_down]
    part = attend(scal, (full,), rest, (1, 6, 3, 5), part)[0]
    mine, theirs = attend(scal, (full,), [kv_x_far], (7,), part, True)
    back = lax.ppermute(theirs, "core", SWAP)
    attended = ((mine + back.astype(F32)) * inv).astype(BF)

    hs, h_last = ring(attended)
    ow_other = [lax.ppermute(w, "core", SWAP) for w in ow]
    o_w = [ow[0], ow_other[0], ow[1], ow_other[1]]
    sums = project_most(scal, hs, o_w, False)
    o_keep, o_send = project_last(scal, 3, h_last, o_w, sums)
    o_got = lax.ppermute(o_send, "xl", SWAP)
    return (o_keep + o_got.astype(F32)).astype(BF)


def solution(mesh):
    split = Mesh(mesh.devices.reshape(4, 2, 2, 2, 8), ("y", "xh", "core", "xl", "z"))
    r, c = ("y", "xh", "core"), ("xl", "z")
    w = ("xh", "core")
    return jax.shard_map(
        shards,
        mesh=split,
        in_specs=(P(r, c), P(r), P(), P(w, c), P(w, None, None, None), P(c), P(w, c)),
        out_specs=P(r, c),
        check_vma=False,
    )
```

```python
import functools
import math

import jax
import jax.numpy as jnp
from jax import lax
from jax.experimental import pallas as pl
from jax.experimental.pallas import tpu as pltpu
from jax.sharding import Mesh
from jax.sharding import PartitionSpec as P


HD = 128
D = 4096
NZ = 8
NY = 4
norm_eps = 1e-06
BF = jnp.bfloat16
F32 = jnp.float32

SWAP = [(0, 1), (1, 0)]
TAKE_0 = [(xl * 2 + xh, xh * 2 + xl) for xh in range(2) for xl in range(2)]
TAKE_1 = [(xl * 2 + 1 - xh, xh * 2 + xl) for xh in range(2) for xl in range(2)]


def shift(x, axis, size, by):
    return lax.ppermute(x, axis, [(i, (i + by) % size) for i in range(size)])


def ring(x):
    got = {0: x}
    up = down = x
    for s in range(1, 4):
        up = got[s] = shift(up, "z", NZ, 1)
        down = got[NZ - s] = shift(down, "z", NZ, -1)
    pairs = [(c * NZ + i, c * NZ + (i + 1 - 2 * c) % NZ) for c in range(2) for i in range(NZ)]
    last = jnp.where(lax.axis_index("core") == 0, up, down)
    return [got[s] for s in range(NZ) if s != 4], lax.ppermute(last, ("core", "z"), pairs)


def proj_kernel(mode, with_squares, n_w, pick, scal, *refs):
    n_x = {"all": 8, "most": 7, "last": 1}[mode]
    xs, refs = refs[:n_x], refs[n_x:]
    n_ws = 4 if mode == "all" else 2 * n_w
    ws, refs = refs[:n_ws], refs[n_ws:]
    z, core = scal[0], scal[1]
    ones = jnp.ones((8, 256), BF)
    dims = (((1,), (1,)), ((), ()))

    def squares_of(x):
        wide = x.astype(F32)
        sq = wide * wide
        hi = sq.astype(BF)
        lo = (sq - hi.astype(F32)).astype(BF)
        return lax.dot_general(ones, hi, dims, preferred_element_type=F32) + lax.dot_general(
            ones, lo, dims, preferred_element_type=F32
        )

    def column(s):
        return pl.multiple_of(lax.rem(z - s + NZ, NZ) * 256, 256)

    def write(acc, keep, send):
        half = acc.shape[1] // 2

        def put(first):
            mine, other = slice(0, half), slice(half, 2 * half)
            if not first:
                mine, other = other, mine
            keep[...] = acc[:, mine]
            send[: keep.shape[0], :] = acc[:, other].astype(BF)

        flag = scal[pick]
        pl.when(flag == 0)(functools.partial(put, True))
        pl.when(flag != 0)(functools.partial(put, False))

    if mode == "last":
        if with_squares:
            sums, old_sq, keep, send, new_sq, rows_scr, acc = refs
        else:
            sums, keep, send, acc = refs
        off = column(4)
        here = off // 1024 == core
        off = pl.multiple_of(lax.rem(off, 1024), 256)
        x = xs[0][...]

        def add(which):
            width = acc.shape[1] // n_w
            for k in range(n_w):
                cols = slice(k * width, (k + 1) * width)
                acc[:, cols] = sums[:, cols] + jnp.dot(
                    x, ws[2 * k + which][pl.ds(off, 256), :], preferred_element_type=F32
                )

        pl.when(here)(functools.partial(add, 0))
        pl.when(jnp.logical_not(here))(functools.partial(add, 1))
        write(acc, keep, send)
        if with_squares:
            rest = old_sq[...] + squares_of(x)
            new_sq[...] = rest
            rows_scr[...] = jnp.zeros_like(rows_scr)
            for t in range(3):
                term = rest.astype(BF).astype(F32)
                for k in range(4):
                    rows_scr[pl.ds(4 * t + k, 1), :] = term[:1, k * HD : (k + 1) * HD]
                rest = rest - term
            send[keep.shape[0] :, :] = rows_scr[...].astype(BF)
        return

    x_scr = refs[-1]
    order = [s for s in range(NZ) if s != 4]
    for s, ref in zip(order, xs):
        x_scr[:, pl.ds(column(s), 256)] = ref[...]
    if mode == "all":
        x_scr[:, pl.ds(column(4), 256)] = xs[7][...]
        keep, send, acc = refs[0], refs[1], refs[-2]
        half = scal[14]
        acc[...] = sum(
            jnp.dot(
                x_scr[:, pl.ds(pl.multiple_of(c * 1024 + h * 512, 512), 512)],
                w[...],
                preferred_element_type=F32,
            )
            for w, c, h in zip(
                ws, (core, core, 1 - core, 1 - core), (half, 1 - half, half, 1 - half)
            )
        )
        write(acc, keep, send)
        return
    x_scr[:, pl.ds(column(4), 256)] = jnp.zeros((x_scr.shape[0], 256), BF)
    acc = refs[0]
    near = pl.multiple_of(core * 1024, 1024)
    far = pl.multiple_of((1 - core) * 1024, 1024)
    width = acc.shape[1] // n_w
    for k in range(n_w):
        acc[:, k * width : (k + 1) * width] = jnp.dot(
            x_scr[:, pl.ds(near, 1024)], ws[2 * k][...], preferred_element_type=F32
        ) + jnp.dot(x_scr[:, pl.ds(far, 1024)], ws[2 * k + 1][...], preferred_element_type=F32)
    if with_squares:
        refs[1][...] = sum(squares_of(ref[...]) for ref in xs)


VM = pl.BlockSpec(memory_space=pltpu.VMEM)
SM = pl.BlockSpec(memory_space=pltpu.SMEM)


def project_most(scal, xs, ws, with_squares):
    rows = xs[0].shape[0]
    n_w = len(ws) // 2
    total = n_w * ws[0].shape[1]
    out = [jax.ShapeDtypeStruct((rows, total), F32)]
    if with_squares:
        out.append(jax.ShapeDtypeStruct((8, rows), F32))
    return pl.pallas_call(
        functools.partial(proj_kernel, "most", with_squares, n_w, None),
        out_shape=out,
        in_specs=[SM] + [VM] * (len(xs) + len(ws)),
        out_specs=[VM] * len(out),
        scratch_shapes=[pltpu.VMEM((rows, 8 * 256), BF)],
        cost_estimate=pl.CostEstimate(
            flops=2 * rows * 1792 * total, transcendentals=0, bytes_accessed=8 * rows * total
        ),
        compiler_params=pltpu.CompilerParams(vmem_limit_bytes=PROJECT_VMEM),
        name="project_most",
    )(scal, *xs, *ws)


def project_last(scal, pick, last, ws, sums):
    rows = last.shape[0]
    n_w = len(ws) // 2
    total = n_w * ws[0].shape[1]
    squares = len(sums) > 1
    out = [
        jax.ShapeDtypeStruct((rows, total // 2), F32),
        jax.ShapeDtypeStruct((rows + 16 if squares else rows, total // 2), BF),
    ]
    scratch = [pltpu.VMEM((rows, total), F32)]
    if squares:
        out.append(jax.ShapeDtypeStruct((8, rows), F32))
        scratch.insert(0, pltpu.VMEM((16, HD), F32))
    return pl.pallas_call(
        functools.partial(proj_kernel, "last", squares, n_w, pick),
        out_shape=out,
        in_specs=[SM] + [VM] * (1 + len(ws) + len(sums)),
        out_specs=[VM] * len(out),
        scratch_shapes=scratch,
        compiler_params=pltpu.CompilerParams(vmem_limit_bytes=PROJECT_VMEM),
        name="project_last",
    )(scal, last, *ws, *sums)


def project_all(scal, pick, xs, last, ws):
    rows = last.shape[0]
    total = ws[0].shape[1]
    out = [
        jax.ShapeDtypeStruct((rows, total // 2), F32),
        jax.ShapeDtypeStruct((rows, total // 2), BF),
    ]
    return pl.pallas_call(
        functools.partial(proj_kernel, "all", False, 1, pick),
        out_shape=out,
        in_specs=[SM] + [VM] * (8 + len(ws)),
        out_specs=[VM] * len(out),
        scratch_shapes=[pltpu.VMEM((rows, total), F32), pltpu.VMEM((rows, 8 * 256), BF)],
        cost_estimate=pl.CostEstimate(
            flops=2 * rows * 2048 * total, transcendentals=0, bytes_accessed=8 * rows * total
        ),
        compiler_params=pltpu.CompilerParams(vmem_limit_bytes=PROJECT_VMEM),
        name="project_all",
    )(scal, *xs, last, *ws)


def scale_kernel(keep, got, squares, out, scale):
    rows = keep.shape[0]
    below = got[rows:, :].astype(F32)
    for k in range(rows // HD):
        at = slice(k * HD, (k + 1) * HD)
        total = squares[:1, at] + below[k : k + 1] + below[4 + k : 5 + k] + below[8 + k : 9 + k]
        row = lax.rsqrt(total * (1.0 / D) + norm_eps)
        column = jnp.broadcast_to(row, (HD, HD)).T
        out[at, :] = ((keep[at, :] + got[at, :].astype(F32)) * column).astype(BF)
        scale[at, :] = jnp.concatenate([column, column], axis=1)


def scale_rows(keep, got, squares):
    rows = keep.shape[0]
    return pl.pallas_call(
        scale_kernel,
        out_shape=[
            jax.ShapeDtypeStruct((rows, HD), BF),
            jax.ShapeDtypeStruct((rows, 2 * HD), F32),
        ],
        in_specs=[VM] * 3,
        out_specs=[VM] * 2,
        compiler_params=pltpu.CompilerParams(vmem_limit_bytes=PROJECT_VMEM),
        name="scale_rows",
    )(keep, got, squares)


PROJECT_VMEM = 10 << 20
ATTEND_VMEM = 16 << 20


def attend_kernel(which, first, final, scal, *refs):
    n = len(which)
    if first:
        coef_ref, q_ref, q_other_ref, *refs = refs
    else:
        q_scr, before, *refs = refs
    kvs, refs = refs[:n], refs[n:]
    if first:
        acc, q_scr, k_scr, v_scr = refs
    elif final:
        own_out, other_out, k_scr, v_scr, acc = refs
    else:
        acc, k_scr, v_scr = refs
    rows = acc.shape[1]

    def one_hot(ref, at):
        ids = ref[rows:, :].astype(F32)[at // 256 : at // 256 + 1, :]
        lane = lax.broadcasted_iota(jnp.int32, (16, 256), 0)
        hot = (ids == (lane % 4).astype(F32)) & (lane < 8)
        unit = lax.broadcasted_iota(jnp.int32, (16, HD), 0) == lax.broadcasted_iota(
            jnp.int32, (16, HD), 1
        )
        return lax.dot_general(
            hot.astype(F32).astype(BF),
            unit.astype(F32).astype(BF),
            (((0,), (0,)), ((), ())),
            preferred_element_type=F32,
        )

    for i in range(n):
        k_scr[i, :, :HD] = kvs[i][:rows, :HD]
        for at in range(0, rows, 256):
            k_scr[i, at : at + 256, HD:] = one_hot(kvs[i], at).astype(BF)
        v_scr[i] = kvs[i][:rows, HD:]
    if first:
        for g, ref in enumerate((q_ref, q_other_ref)):
            for at in range(0, rows, 256):
                hot = one_hot(ref, at)
                for h in range(2):
                    q_scr[g, h, at : at + 256, HD:] = (hot * coef_ref[h : h + 1, :]).astype(BF)
            for h in range(2):
                q_scr[g, h, :, :HD] = ref[:rows, h * HD : (h + 1) * HD]
        acc[...] = jnp.zeros_like(acc)
    else:
        acc[...] = before[...]

    def tile(g, i, ahead=None):
        keys = k_scr[i]
        values = v_scr[i]
        for h in range(2):
            u = lax.dot_general(
                q_scr[g, h], keys, (((1,), (1,)), ((), ())), preferred_element_type=F32
            )
            w = u + u * jnp.tanh(u)
            if ahead is not None:
                t_at = lax.broadcasted_iota(jnp.int32, w.shape, 0)
                u_at = lax.broadcasted_iota(jnp.int32, w.shape, 1)
                w = jnp.where(u_at - t_at <= ahead, w, 0.0)
            acc[g, :, h * HD : (h + 1) * HD] += jnp.dot(
                w.astype(BF), values, preferred_element_type=F32
            )

    def place_of(i):
        at = scal[6 + which[0]]
        for m in range(1, n):
            at = jnp.where(i == m, scal[6 + which[m]], at)
        return at

    if first:

        def one(k, carry):
            g, i = k // n, lax.rem(k, n)

            @pl.when(jnp.logical_or(k == 0, place_of(i) < scal[4 + g]))
            def _():
                tile(g, i, jnp.where(k == 0, 0, rows))

            return carry

        lax.fori_loop(0, 2 * n, one, 0)
    else:

        def both(i, carry):
            @pl.when(place_of(i) < scal[4])
            def _():
                tile(0, i)
                tile(1, i)

            return carry

        lax.fori_loop(0, n, both, 0)
    if final:
        own_out[...] = acc[0]
        other_out[...] = acc[1].astype(BF)


def attend(scal, queries, kvs, which, before=None, final=False):
    rows = kvs[0].shape[0] - 16
    n = len(kvs)
    first = before is None
    out = [jax.ShapeDtypeStruct((2, rows, 2 * HD), F32)]
    scratch = [pltpu.VMEM((n, rows, 2 * HD), BF), pltpu.VMEM((n, rows, HD), BF)]
    if first:
        out.append(jax.ShapeDtypeStruct((2, 2, rows, 2 * HD), BF))
    if final:
        out = [
            jax.ShapeDtypeStruct((rows, 2 * HD), F32),
            jax.ShapeDtypeStruct((rows, 2 * HD), BF),
        ]
        scratch.append(pltpu.VMEM((2, rows, 2 * HD), F32))
    ins = [*queries] if first else [*queries, before]
    return pl.pallas_call(
        functools.partial(attend_kernel, which, first, final),
        out_shape=out,
        in_specs=[SM] + [VM] * (len(ins) + n),
        out_specs=[VM] * len(out),
        scratch_shapes=scratch,
        cost_estimate=pl.CostEstimate(
            flops=n * 2 * 4 * 2 * rows * rows * 256, transcendentals=0, bytes_accessed=1 << 20
        ),
        compiler_params=pltpu.CompilerParams(vmem_limit_bytes=ATTEND_VMEM),
        name="attend",
    )(scal, *ins, *kvs)


def shards(events, domain_ids, block_order, query_weight, keyval_weight, head_bias, out_weight):
    rows = events.shape[0]
    y, xh, core = lax.axis_index("y"), lax.axis_index("xh"), lax.axis_index("core")
    xl, z = lax.axis_index("xl"), lax.axis_index("z")
    chip_x = ("xh", "xl")

    xs, last = ring(events)
    pairs = [
        lax.dynamic_slice(
            keyval_weight, (0, z // 2 + 4 * b, z % 2, 0), (keyval_weight.shape[0], 1, 1, HD)
        ).reshape(-1, HD)
        for b in range(2)
    ]
    kvw = lax.ppermute(jnp.concatenate(pairs, axis=1), chip_x, TAKE_0)
    half = query_weight.shape[0] // 2
    qw_in = lax.dynamic_slice_in_dim(query_weight, (y % 2) * half, half, 0)
    qw = [lax.ppermute(qw_in, chip_x, t) for t in (TAKE_0, TAKE_1)]

    ids = jnp.pad(domain_ids.astype(BF).reshape(2, 256), ((0, 14), (0, 0)))
    lane = jnp.arange(HD, dtype=jnp.int32)
    bias = 0.5 * head_bias
    high = lax.reduce_precision(bias, 8, 7)
    coef = jnp.where(lane < 4, high[:, None], jnp.where(lane < 8, (bias - high)[:, None], 0.0))

    dy = jnp.array([0, 0, 1, 1, 3, 3, 2, 2], jnp.int32)
    dx = jnp.array([0, 1] * 4, jnp.int32)
    src_y = (y - dy) % NY
    at = jnp.sum(jnp.where(src_y[:, None] == jnp.arange(NY), block_order[None, :], 0), axis=1)
    key_at = at * 4 + (xh ^ dx) * 2 + core
    own_at = key_at[0]
    scal = jnp.concatenate([jnp.stack([z, core, xl, xl ^ xh, own_at, own_at ^ 1]), key_at, (y % 2)[None]])
    place = own_at * rows + jnp.arange(rows, dtype=jnp.int32)
    inv = lax.rsqrt((place + 1).astype(F32))[:, None]

    kvw_other = lax.ppermute(kvw, "core", SWAP)
    kv_w = [kvw, kvw_other]
    sums = project_most(scal, xs, kv_w, True)
    kv_keep, kv_send, squares = project_last(scal, 2, last, kv_w, sums)
    kv_got = lax.ppermute(kv_send, "xl", SWAP)
    mine, row_scale = scale_rows(kv_keep, kv_got, squares)
    other = lax.ppermute(mine, "z", [(i, i ^ 1) for i in range(NZ)])
    even = z % 2 == 0
    kv = jnp.concatenate([jnp.where(even, mine, other), jnp.where(even, other, mine)], axis=1)
    kv = jnp.concatenate([kv, ids], axis=0)
    kv_x = lax.ppermute(kv, "xh", SWAP)
    kv_up = shift(kv, "y", NY, 1)
    kv_down = shift(kv, "y", NY, -1)
    kv_far = shift(kv_up, "y", NY, 1)
    kv_x_up = shift(kv_x, "y", NY, 1)
    kv_x_down = shift(kv_x, "y", NY, -1)
    kv_x_far = shift(kv_x_down, "y", NY, -1)

    qw = jnp.concatenate(lax.optimization_barrier((*qw, kv_send))[:2], axis=1)
    q_w = [qw, lax.ppermute(qw, "y", [(i, i ^ 1) for i in range(NY)])]
    q_w += [lax.ppermute(w, "core", SWAP) for w in q_w]
    q_keep, q_send = project_all(scal, 3, xs, last, q_w)
    q_got = lax.ppermute(q_send, "xl", SWAP)
    q = ((q_keep + q_got.astype(F32)) * (row_scale * (0.5 / math.sqrt(HD)))).astype(BF)
    q = jnp.concatenate([q, lax.optimization_barrier(ids)], axis=0)
    q_other = lax.ppermute(q, "core", SWAP)

    ow = [lax.ppermute(out_weight, chip_x, t) for t in (TAKE_0, TAKE_1)]

    part, full = attend(scal, (coef, q, q_other), [kv, kv_up], (0, 2))
    rest = [kv_down, kv_x, kv_far, kv_x_up, kv_x_down]
    part = attend(scal, (full,), rest, (4, 1, 6, 3, 5), part)[0]
    mine, theirs = attend(scal, (full,), [kv_x_far], (7,), part, True)
    back = lax.ppermute(theirs, "core", SWAP)
    attended = ((mine + back.astype(F32)) * inv).astype(BF)

    hs, h_last = ring(attended)
    ow_other = [lax.ppermute(w, "core", SWAP) for w in ow]
    o_w = [ow[0], ow_other[0], ow[1], ow_other[1]]
    sums = project_most(scal, hs, o_w, False)
    o_keep, o_send = project_last(scal, 3, h_last, o_w, sums)
    o_got = lax.ppermute(o_send, "xl", SWAP)
    return (o_keep + o_got.astype(F32)).astype(BF)


def solution(mesh):
    split = Mesh(mesh.devices.reshape(4, 2, 2, 2, 8), ("y", "xh", "core", "xl", "z"))
    r, c = ("y", "xh", "core"), ("xl", "z")
    w = ("xh", "core")
    return jax.shard_map(
        shards,
        mesh=split,
        in_specs=(P(r, c), P(r), P(), P(w, c), P(w, None, None, None), P(c), P(w, c)),
        out_specs=P(r, c),
        check_vma=False,
    )
```
